32 devices in a mesh: segment: 4 (over x, core), seq: 2 (over y), rep: 4 (over z).
Axes of the slice: x: 2, y: 2, z: 4, core: 2. Of those that a mesh axis runs over, the one named last changes fastest.
Arguments:
- query: bfloat16 [4, 384, 5120], P('segment', ('rep', 'seq')), parts along dimension 1, may hold values from -7 to 7
- key_new: bfloat16 [4, 384, 5120], P('segment', ('rep', 'seq')), parts along dimension 1, may hold values from -4 to 4
- value_new: bfloat16 [4, 384, 5120], P('segment', ('rep', 'seq')), parts along dimension 1, may hold values from -4 to 4
- stale_key: bfloat16 [4, 160, 192, 128], P('segment', ('rep', 'seq')), parts along dimension 1, may hold values from -12 to 12
- stale_value: bfloat16 [4, 160, 192, 128], P('segment', ('rep', 'seq')), parts along dimension 1, may hold values from -4 to 4
- head_order: int32 [40], replicated, may hold values from 0 to 39, each once
- tick: int32 [1], replicated, may hold values from 0 to 8191
Outputs:
- handoff: bfloat16 [4, 384, 5120], P('segment', ('rep', 'seq')), parts along dimension 1
The draws below stay inside these ranges and needn't reach their ends.
There are 4 independent parts, one for each index of `rep`. The reference program is written for one: setup_inputs(seed, part) draws one part's arguments, and reference() takes and returns one part's arrays. A program takes and returns all parts, laid end to end along the dimension named above; an argument that names none is the same for every part. Nothing has to cross between parts.
Inputs may be any that keep to these rules, and one draw needn't show every extreme that they name: `head_order`: every head appears once. `tick`: only its value modulo 2 matters.
All inputs are finite; a program needn't handle non-finite values.
Results may differ from the reference program's by a relative error of at most 0.0044.
Values may be sent and summed in bfloat16 or wider, within the bound.
No kernel may reach another device: no remote copies, remote signals or barrier semaphores. Data moves between devices by JAX's collectives and lax.ppermute only.
A program may use at most 64 MiB of HBM per device.

```python
import jax
import jax.numpy as jnp
from jax import lax

HEADS = 40
HD = 128
D = 5120
MICRO = 2
SEGMENTS = 4
GROUP = 2
PATCH_TOK = 96
LENGTH = 192
HEADS_DEV = 20
SLOTS = 40


def draw_query(key, part):
    shape = (SEGMENTS, PATCH_TOK, D)
    values = jax.random.truncated_normal(jax.random.fold_in(key, 1), -6.0, 6.0, shape)
    return values.astype(jnp.bfloat16)


def draw_stale_key(key, part):
    shape = (SEGMENTS, SLOTS, LENGTH, HD)
    values = jax.random.truncated_normal(jax.random.fold_in(key, 3), -4.0, 4.0, shape)
    return values.astype(jnp.bfloat16)


def block_levels(stream_key, dims, cuts, smallest, high):
    def one(position, parts):
        heights = jax.random.uniform(jax.random.fold_in(jax.random.fold_in(stream_key, 6), position), (parts,), jnp.float32, smallest / len(cuts), high / len(cuts))
        return jnp.repeat(jnp.exp(heights), dims[position] // parts).reshape((-1,) + (1,) * (len(dims) - position - 1))

    factor_of = one(*cuts[0])
    for cut in cuts[1:]:
        factor_of = factor_of * one(*cut)
    return factor_of


def noise(key, dims, width, limit, pieces=(), kind=jnp.bfloat16):
    entries = width * jax.random.normal(key, dims, jnp.float32)
    if pieces:
        entries = entries * block_levels(key, dims, pieces, -0.22, 0.18)
    return jnp.clip(entries, -limit, limit).astype(kind)


def setup_inputs(seed: int = 0, part: int = 0) -> dict:
    key_of = jax.random.split(jax.random.key(seed), 8)
    part_splits = jax.random.split(jax.random.fold_in(key_of[7], part), 8)
    query = draw_query(jax.random.fold_in(jax.random.fold_in(key_of[7], part), 71), part)
    key_new = noise(part_splits[1], (SEGMENTS, PATCH_TOK, D), 1.0, 4.0, ((0, 4), (1, 2)))
    value_new = noise(part_splits[2], (SEGMENTS, PATCH_TOK, D), 1.0, 4.0, ((0, 4), (1, 2)))
    stale_key = draw_stale_key(jax.random.fold_in(jax.random.fold_in(key_of[7], part), 71), part)
    stale_value = noise(part_splits[4], (SEGMENTS, SLOTS, LENGTH, HD), 1.0, 4.0, ((0, 4), (1, 2)))
    head_order = jax.random.permutation(key_of[5], HEADS).astype(jnp.int32)
    tick = jax.random.randint(key_of[6], (1,), 0, 4096 * MICRO).astype(jnp.int32)
    return {"query": query, "key_new": key_new, "value_new": value_new, "stale_key": stale_key, "stale_value": stale_value, "head_order": head_order, "tick": tick}


def reference(query, key_new, value_new, stale_key, stale_value, head_order, tick):
    score_scale = HD ** -0.5
    unit_ids = jnp.arange(HEADS, dtype=jnp.int32)
    slot_ids = ((unit_ids % GROUP) * HEADS_DEV + unit_ids // GROUP).astype(jnp.int32)
    results = []
    for segment_id in range(SEGMENTS):
        patch_index = ((tick[0] - segment_id) % MICRO).astype(jnp.int32)
        first_row = (patch_index * PATCH_TOK).astype(jnp.int32)
        query_heads = query[segment_id].reshape(PATCH_TOK, HEADS, HD)
        key_heads = key_new[segment_id].reshape(PATCH_TOK, HEADS, HD)
        value_heads = value_new[segment_id].reshape(PATCH_TOK, HEADS, HD)
        stale_keys = stale_key[segment_id]
        stale_values = stale_value[segment_id]

        def one_head(pair):
            head_id, slot_id = pair
            query_rows = query_heads[:, head_id, :]
            key_rows = lax.dynamic_update_slice(stale_keys[slot_id], key_heads[:, head_id, :], (first_row, jnp.int32(0)))
            value_rows = lax.dynamic_update_slice(stale_values[slot_id], value_heads[:, head_id, :], (first_row, jnp.int32(0)))
            scores = jnp.dot(query_rows, key_rows.T, preferred_element_type=jnp.float32) * score_scale
            top = jnp.max(scores, axis=-1, keepdims=True)
            weights = jnp.exp(scores - top).astype(jnp.bfloat16)
            total = jnp.sum(weights.astype(jnp.float32), axis=-1, keepdims=True)
            numer = jnp.dot(weights, value_rows, preferred_element_type=jnp.float32)
            return (numer / total).astype(jnp.bfloat16)

        attended = lax.map(one_head, (head_order, slot_ids))
        placed = jnp.zeros((PATCH_TOK, HEADS, HD), jnp.bfloat16).at[:, head_order, :].set(jnp.transpose(attended, (1, 0, 2)))
        results.append(placed.reshape(PATCH_TOK, D))
    stacked = jnp.stack(results, axis=0)
    return jnp.roll(stacked, 1, axis=0)
```

```python
import functools

import jax
import jax.numpy as jnp
from jax import lax
from jax.experimental import pallas as pl
from jax.experimental.pallas import tpu as pltpu
from jax.sharding import PartitionSpec as P

MICRO = 2
CHUNKS = 1
KERNEL_VMEM = 16 << 20


def from_behind(block, axis, distance):
    devices = range(lax.axis_size(axis))
    route = [((i - distance) % len(devices), i) for i in devices]
    return lax.ppermute(block, axis, route)


def select_table(head_order, group_size, heads_dev):
    head_count = head_order.shape[0]
    slot_ids = (
        jnp.arange(heads_dev, dtype=jnp.int32)[None, :] * group_size
        + jnp.arange(group_size, dtype=jnp.int32)[:, None]
    )
    head_ids = jnp.arange(head_count, dtype=jnp.int32)
    matches = slot_ids[:, :, None] == head_ids[None, None, :]
    head_of = jnp.sum(jnp.where(matches, head_order[None, None, :], 0), axis=-1)
    head_of = jnp.where(slot_ids < head_count, head_of, -1)
    return (head_of[:, :, None] == head_ids[None, None, :]).astype(jnp.bfloat16)


def pack_heads(table, values, head_size):
    rows = values.shape[1]
    per_head = values[0].reshape(rows, table.shape[2], head_size)
    return jnp.einsum("dlh,thc->tdlc", table, per_head, preferred_element_type=jnp.float32).astype(
        jnp.bfloat16
    )


def head_major(received):
    return jnp.transpose(received[:, 0], (1, 0, 2))


def block_count(patch_tok):
    count = max(1, patch_tok // 512)
    while patch_tok % count != 0:
        count = count - 1
    return count


def wide_group(query, key_new, value_new, stale_key, stale_value, head_order, tick):
    group_size = lax.axis_size("seq")
    heads_dev = stale_key.shape[1]
    head_size = stale_key.shape[3]
    tok_rows = query.shape[1]
    patch_tok = tok_rows * group_size
    blocks = block_count(patch_tok)
    block_rows = patch_tok // blocks
    score_scale = head_size ** (-0.5)
    table = select_table(head_order, group_size, heads_dev)
    patch_index = (tick[0] - lax.axis_index("segment")) % MICRO
    first_row = patch_index * patch_tok

    def with_fresh(stale_buf, fresh_rows):
        return lax.dynamic_update_slice(
            stale_buf[0], fresh_rows, (jnp.int32(0), first_row, jnp.int32(0))
        )

    sent_query, sent_key, sent_value = (
        lax.all_to_all(
            pack_heads(table, part, head_size), "seq", split_axis=1, concat_axis=0, tiled=True
        )
        for part in (query, key_new, value_new)
    )
    key_buf = with_fresh(stale_key, head_major(sent_key))
    value_buf = with_fresh(stale_value, head_major(sent_value))

    def attend_full(operands):
        query_blocks, key_rows, value_rows = operands

        def one_block(query_rows):
            scores = (
                jnp.dot(query_rows, key_rows.T, preferred_element_type=jnp.float32) * score_scale
            )
            top = jnp.max(scores, axis=-1, keepdims=True)
            weights = jnp.exp(scores - top).astype(jnp.bfloat16)
            total = jnp.sum(weights, axis=-1, keepdims=True, dtype=jnp.float32)
            numer = jnp.dot(weights, value_rows, preferred_element_type=jnp.float32)
            return (numer / total).astype(jnp.bfloat16)

        return lax.map(one_block, query_blocks).reshape(patch_tok, head_size)

    heads_rows = head_major(sent_query)
    attended = lax.map(
        attend_full,
        (
            heads_rows.reshape(heads_rows.shape[0], blocks, block_rows, heads_rows.shape[-1]),
            key_buf,
            value_buf,
        ),
    )
    outgoing = jnp.transpose(attended, (1, 0, 2))[:, None, :, :]
    returned = lax.all_to_all(outgoing, "seq", split_axis=0, concat_axis=1, tiled=True)
    merged = jnp.einsum(
        "dlh,tdlc->thc", table, returned, preferred_element_type=jnp.float32
    ).astype(jnp.bfloat16)
    result = merged.reshape(1, tok_rows, table.shape[2] * head_size)
    return from_behind(result, "segment", 1)


def any_space():
    return pl.BlockSpec(memory_space=pl.ANY)


def scalar_space():
    return pl.BlockSpec(memory_space=pltpu.SMEM)


def columns_of(order_ref, unit, head_size):
    return pl.ds(pl.multiple_of(order_ref[unit] * head_size, head_size), head_size)


def pack_body(low, heads, order_ref, query_ref, key_ref, value_ref, out_ref, sem):
    other = 1 - lax.axis_index("seq")
    head_size = out_ref.shape[3]
    for l in range(heads):
        columns = columns_of(order_ref, 2 * (low + l) + other, head_size)
        for place, source in enumerate((key_ref, value_ref, query_ref)):
            pltpu.make_async_copy(source.at[0, :, columns], out_ref.at[place, l], sem).start()
    pltpu.make_async_copy(out_ref, out_ref, sem).wait()


def pack(low, heads, head_order, query, key_new, value_new):
    tok_rows = query.shape[1]
    head_size = query.shape[2] // head_order.shape[0]
    shape = (3, heads, tok_rows, head_size)
    return pl.pallas_call(
        functools.partial(pack_body, low, heads),
        out_shape=jax.ShapeDtypeStruct(shape, query.dtype),
        in_specs=[scalar_space()] + [any_space()] * 3,
        out_specs=any_space(),
        scratch_shapes=[pltpu.SemaphoreType.DMA],
        cost_estimate=pl.CostEstimate(
            flops=0, bytes_accessed=12 * heads * tok_rows * head_size, transcendentals=0
        ),
        compiler_params=pltpu.CompilerParams(vmem_limit_bytes=KERNEL_VMEM),
        name="pack",
    )(head_order, query, key_new, value_new)


def attend_body(
    low,
    heads,
    order_ref,
    tick_ref,
    query_ref,
    key_ref,
    value_ref,
    recv_ref,
    stale_key_ref,
    stale_value_ref,
    near_ref,
    far_ref,
    query_buf,
    key_buf,
    value_buf,
    sems,
):
    me = lax.axis_index("seq")
    tok_rows, head_size = near_ref.shape[1:]
    patch_tok = 2 * tok_rows
    kept = (tick_ref[0] - lax.axis_index("segment") + 1) & 1
    kept_rows = pl.ds(pl.multiple_of(kept * patch_tok, patch_tok), patch_tok)
    group = pl.ds(low, heads)
    columns = pl.ds(0, head_size)
    own = pl.ds(patch_tok, tok_rows)
    got = pl.ds(patch_tok + tok_rows, tok_rows)
    key_sem, value_sem, query_sem = sems.at[0], sems.at[1], sems.at[2]

    pltpu.make_async_copy(
        stale_key_ref.at[0, group, kept_rows], key_buf.at[:, pl.ds(0, patch_tok)], key_sem
    ).start()
    pltpu.make_async_copy(
        stale_value_ref.at[0, group, kept_rows],
        value_buf.at[:, pl.ds(0, patch_tok), columns],
        value_sem,
    ).start()
    pltpu.make_async_copy(recv_ref.at[0], key_buf.at[:, got], key_sem).start()
    pltpu.make_async_copy(recv_ref.at[1], value_buf.at[:, got, columns], value_sem).start()
    pltpu.make_async_copy(
        recv_ref.at[2], query_buf.at[:, pl.ds(tok_rows, tok_rows)], query_sem
    ).start()
    for l in range(heads):
        head = columns_of(order_ref, 2 * (low + l) + me, head_size)
        pltpu.make_async_copy(key_ref.at[0, :, head], key_buf.at[l, own], key_sem).start()
        pltpu.make_async_copy(
            query_ref.at[0, :, head], query_buf.at[l, pl.ds(0, tok_rows)], query_sem
        ).start()
        pltpu.make_async_copy(
            value_ref.at[0, :, head], value_buf.at[l, own, columns], value_sem
        ).start()
    value_buf[:, :, head_size:] = jnp.ones(
        (heads, value_buf.shape[1], head_size), value_buf.dtype
    )
    pltpu.make_async_copy(query_buf, query_buf, query_sem).wait()
    pltpu.make_async_copy(key_buf, key_buf, key_sem).wait()
    pltpu.make_async_copy(
        value_buf.at[:, :, columns], value_buf.at[:, :, columns], value_sem
    ).wait()

    factor = head_size ** (-0.5) * 1.4426950408889634
    for l in range(heads):
        scores = lax.dot_general(
            query_buf[l], key_buf[l], (((1,), (1,)), ((), ())), preferred_element_type=jnp.float32
        )
        top = jnp.max(scores, axis=-1, keepdims=True)
        weights = jnp.exp2((scores - top) * factor).astype(jnp.bfloat16)
        both = jnp.dot(weights, value_buf[l], preferred_element_type=jnp.float32)
        result = (both[:, :head_size] / both[:, head_size:]).astype(near_ref.dtype)
        near_ref[l] = result[:tok_rows]
        far_ref[l] = result[tok_rows:]


def attend(low, heads, head_order, tick, query, key_new, value_new, received, stale_key, stale_value):
    tok_rows = query.shape[1]
    length, head_size = stale_key.shape[2:]
    out = jax.ShapeDtypeStruct((heads, tok_rows, head_size), query.dtype)
    return pl.pallas_call(
        functools.partial(attend_body, low, heads),
        out_shape=(out, out),
        in_specs=[scalar_space()] * 2 + [any_space()] * 6,
        out_specs=(pl.BlockSpec(memory_space=pltpu.VMEM),) * 2,
        scratch_shapes=[
            pltpu.VMEM((heads, 2 * tok_rows, head_size), query.dtype),
            pltpu.VMEM((heads, length, head_size), query.dtype),
            pltpu.VMEM((heads, length, 2 * head_size), query.dtype),
            pltpu.SemaphoreType.DMA((3,)),
        ],
        cost_estimate=pl.CostEstimate(
            flops=12 * heads * tok_rows * length * head_size,
            bytes_accessed=2 * heads * head_size * (2 * length + 4 * tok_rows),
            transcendentals=2 * heads * tok_rows * length,
        ),
        compiler_params=pltpu.CompilerParams(vmem_limit_bytes=KERNEL_VMEM),
        name="attend",
    )(head_order, tick, query, key_new, value_new, received, stale_key, stale_value)


def unpack_body(bounds, order_ref, *refs):
    count = len(bounds)
    near, far = refs[:count], refs[count : 2 * count]
    out_ref, sem = refs[2 * count :]
    me = lax.axis_index("seq")
    head_size = near[0].shape[2]
    for c, (low, heads) in enumerate(bounds):
        for l in range(heads):
            for side, source in ((me, near[c]), (1 - me, far[c])):
                columns = columns_of(order_ref, 2 * (low + l) + side, head_size)
                pltpu.make_async_copy(source.at[l], out_ref.at[0, :, columns], sem).start()
    pltpu.make_async_copy(out_ref, out_ref, sem).wait()


def unpack(bounds, head_order, near, far):
    tok_rows, head_size = near[0].shape[1:]
    shape = (1, tok_rows, head_order.shape[0] * head_size)
    return pl.pallas_call(
        functools.partial(unpack_body, bounds),
        out_shape=jax.ShapeDtypeStruct(shape, near[0].dtype),
        in_specs=[scalar_space()] + [any_space()] * (2 * len(bounds)),
        out_specs=any_space(),
        scratch_shapes=[pltpu.SemaphoreType.DMA],
        cost_estimate=pl.CostEstimate(
            flops=0, bytes_accessed=4 * shape[1] * shape[2], transcendentals=0
        ),
        compiler_params=pltpu.CompilerParams(vmem_limit_bytes=KERNEL_VMEM),
        name="unpack",
    )(head_order, *near, *far)


def pair_group(query, key_new, value_new, stale_key, stale_value, head_order, tick):
    heads_dev = stale_key.shape[1]
    segments = lax.axis_size("segment")
    edges = [heads_dev * c // CHUNKS for c in range(CHUNKS + 1)]
    bounds = [(a, b - a) for a, b in zip(edges[:-1], edges[1:])]
    ahead = [(s, (s + 1) % segments) for s in range(segments)]
    across = [(2 * s + j, 2 * t + 1 - j) for s, t in ahead for j in range(2)]

    received = []
    for low, heads in bounds:
        packed = pack(low, heads, head_order, query, key_new, value_new)
        received.append(lax.ppermute(packed, "seq", [(0, 1), (1, 0)]))
    near, far = [], []
    for (low, heads), got in zip(bounds, received):
        kept, crossed = attend(
            low, heads, head_order, tick, query, key_new, value_new, got, stale_key, stale_value
        )
        far.append(lax.ppermute(crossed, ("segment", "seq"), across))
        near.append(lax.ppermute(kept, "segment", ahead))
    return unpack(bounds, head_order, near, far)


def per_device(query, key_new, value_new, stale_key, stale_value, head_order, tick):
    group_size = lax.axis_size("seq")
    heads = head_order.shape[0]
    tok_rows, head_size = query.shape[1], stale_key.shape[3]
    paired = (
        group_size == 2
        and heads == 2 * stale_key.shape[1]
        and stale_key.shape[2] == MICRO * 2 * tok_rows
        and tok_rows % 16 == 0
        and head_size % 128 == 0
    )
    chosen = pair_group if paired else wide_group
    return chosen(query, key_new, value_new, stale_key, stale_value, head_order, tick)


def solution(mesh):
    return jax.shard_map(
        per_device,
        mesh=mesh,
        in_specs=(
            P("segment", ("rep", "seq"), None),
            P("segment", ("rep", "seq"), None),
            P("segment", ("rep", "seq"), None),
            P("segment", ("rep", "seq"), None, None),
            P("segment", ("rep", "seq"), None, None),
            P(),
            P(),
        ),
        out_specs=P("segment", ("rep", "seq"), None),
        check_vma=False,
    )
```

```python
import functools

import jax
import jax.numpy as jnp
from jax import lax
from jax.experimental import pallas as pl
from jax.experimental.pallas import tpu as pltpu
from jax.sharding import PartitionSpec as P

MICRO = 2
EDGES = (0, 0.7, 1)
KERNEL_VMEM = 8 << 20


def from_behind(block, axis, distance):
    devices = range(lax.axis_size(axis))
    route = [((i - distance) % len(devices), i) for i in devices]
    return lax.ppermute(block, axis, route)


def select_table(head_order, group_size, heads_dev):
    head_count = head_order.shape[0]
    slot_ids = (
        jnp.arange(heads_dev, dtype=jnp.int32)[None, :] * group_size
        + jnp.arange(group_size, dtype=jnp.int32)[:, None]
    )
    head_ids = jnp.arange(head_count, dtype=jnp.int32)
    matches = slot_ids[:, :, None] == head_ids[None, None, :]
    head_of = jnp.sum(jnp.where(matches, head_order[None, None, :], 0), axis=-1)
    head_of = jnp.where(slot_ids < head_count, head_of, -1)
    return (head_of[:, :, None] == head_ids[None, None, :]).astype(jnp.bfloat16)


def pack_heads(table, values, head_size):
    rows = values.shape[1]
    per_head = values[0].reshape(rows, table.shape[2], head_size)
    return jnp.einsum("dlh,thc->tdlc", table, per_head, preferred_element_type=jnp.float32).astype(
        jnp.bfloat16
    )


def head_major(received):
    return jnp.transpose(received[:, 0], (1, 0, 2))


def block_count(patch_tok):
    count = max(1, patch_tok // 512)
    while patch_tok % count != 0:
        count = count - 1
    return count


def wide_group(query, key_new, value_new, stale_key, stale_value, head_order, tick):
    group_size = lax.axis_size("seq")
    heads_dev = stale_key.shape[1]
    head_size = stale_key.shape[3]
    tok_rows = query.shape[1]
    patch_tok = tok_rows * group_size
    blocks = block_count(patch_tok)
    block_rows = patch_tok // blocks
    score_scale = head_size ** (-0.5)
    table = select_table(head_order, group_size, heads_dev)
    patch_index = (tick[0] - lax.axis_index("segment")) % MICRO
    first_row = patch_index * patch_tok

    def with_fresh(stale_buf, fresh_rows):
        return lax.dynamic_update_slice(
            stale_buf[0], fresh_rows, (jnp.int32(0), first_row, jnp.int32(0))
        )

    sent_query, sent_key, sent_value = (
        lax.all_to_all(
            pack_heads(table, part, head_size), "seq", split_axis=1, concat_axis=0, tiled=True
        )
        for part in (query, key_new, value_new)
    )
    key_buf = with_fresh(stale_key, head_major(sent_key))
    value_buf = with_fresh(stale_value, head_major(sent_value))

    def attend_full(operands):
        query_blocks, key_rows, value_rows = operands

        def one_block(query_rows):
            scores = (
                jnp.dot(query_rows, key_rows.T, preferred_element_type=jnp.float32) * score_scale
            )
            top = jnp.max(scores, axis=-1, keepdims=True)
            weights = jnp.exp(scores - top).astype(jnp.bfloat16)
            total = jnp.sum(weights, axis=-1, keepdims=True, dtype=jnp.float32)
            numer = jnp.dot(weights, value_rows, preferred_element_type=jnp.float32)
            return (numer / total).astype(jnp.bfloat16)

        return lax.map(one_block, query_blocks).reshape(patch_tok, head_size)

    heads_rows = head_major(sent_query)
    attended = lax.map(
        attend_full,
        (
            heads_rows.reshape(heads_rows.shape[0], blocks, block_rows, heads_rows.shape[-1]),
            key_buf,
            value_buf,
        ),
    )
    outgoing = jnp.transpose(attended, (1, 0, 2))[:, None, :, :]
    returned = lax.all_to_all(outgoing, "seq", split_axis=0, concat_axis=1, tiled=True)
    merged = jnp.einsum(
        "dlh,tdlc->thc", table, returned, preferred_element_type=jnp.float32
    ).astype(jnp.bfloat16)
    result = merged.reshape(1, tok_rows, table.shape[2] * head_size)
    return from_behind(result, "segment", 1)


def hbm_space():
    return pl.BlockSpec(memory_space=pltpu.HBM)


def in_hbm(array):
    return pltpu.with_memory_space_constraint(array, pltpu.HBM)


def vmem_space():
    return pl.BlockSpec(memory_space=pltpu.VMEM)


def scalar_space():
    return pl.BlockSpec(memory_space=pltpu.SMEM)


def columns_of(order_ref, unit, head_size):
    return pl.ds(pl.multiple_of(order_ref[unit] * head_size, head_size), head_size)


def moved(count):
    return pl.CostEstimate(flops=0, bytes_accessed=2 * count, transcendentals=0)


def pack_body(bounds, given_ref, query_ref, key_ref, value_ref, order_ref, own_ref, *refs):
    send_refs, (buf, sems) = refs[: len(bounds)], refs[len(bounds) :]
    me = lax.axis_index("seq")
    head_size = own_ref.shape[3]
    copies = [
        pltpu.make_async_copy(source.at[0], buf.at[place], sems.at[place])
        for place, source in enumerate((key_ref, value_ref, query_ref))
    ] + [pltpu.make_async_copy(given_ref, order_ref, sems.at[3])]
    for copy in copies:
        copy.start()
    for copy in copies:
        copy.wait()
    for (low, heads), send_ref in zip(bounds, send_refs):
        for l in range(heads):
            columns = columns_of(order_ref, 2 * (low + l) + 1 - me, head_size)
            for place in range(3):
                send_ref[place, l] = buf[place, :, columns]
    for l in range(own_ref.shape[1]):
        columns = columns_of(order_ref, 2 * l + me, head_size)
        for place in range(3):
            own_ref[place, l] = buf[place, :, columns]


def pack(bounds, head_order, query, key_new, value_new):
    tok_rows, width = query.shape[1:]
    head_size = width // head_order.shape[0]
    own = sum(heads for _, heads in bounds)
    shapes = [pltpu.SMEM(head_order.shape, head_order.dtype)] + [
        jax.ShapeDtypeStruct((3, heads, tok_rows, head_size), query.dtype)
        for heads in [own] + [heads for _, heads in bounds]
    ]
    order, own, *sends = pl.pallas_call(
        functools.partial(pack_body, bounds),
        out_shape=shapes,
        in_specs=[hbm_space()] * 4,
        out_specs=[scalar_space()] + [vmem_space()] * (len(shapes) - 1),
        scratch_shapes=[
            pltpu.VMEM((3, tok_rows, width), query.dtype),
            pltpu.SemaphoreType.DMA((4,)),
        ],
        cost_estimate=moved(6 * tok_rows * width),
        compiler_params=pltpu.CompilerParams(vmem_limit_bytes=KERNEL_VMEM),
        name="pack",
    )(*(in_hbm(x) for x in (head_order, query, key_new, value_new)))
    return order, own, sends


def keep_body(tick_ref, stale_key_ref, stale_value_ref, key_ref, value_ref, sems):
    patch_tok = key_ref.shape[1]
    kept = (tick_ref[0] - lax.axis_index("segment") + 1) & 1
    rows = pl.ds(pl.multiple_of(kept * patch_tok, patch_tok), patch_tok)
    copies = [
        pltpu.make_async_copy(source.at[0, :, rows], target, sems.at[i])
        for i, (source, target) in enumerate(
            ((stale_key_ref, key_ref), (stale_value_ref, value_ref))
        )
    ]
    for copy in copies:
        copy.start()
    for copy in copies:
        copy.wait()


def keep(tick, stale_key, stale_value):
    _, heads, length, head_size = stale_key.shape
    kept = jax.ShapeDtypeStruct((heads, length // MICRO, head_size), stale_key.dtype)
    return pl.pallas_call(
        keep_body,
        out_shape=(kept, kept),
        in_specs=[scalar_space()] + [hbm_space()] * 2,
        out_specs=(vmem_space(),) * 2,
        scratch_shapes=[pltpu.SemaphoreType.DMA((2,))],
        cost_estimate=moved(2 * heads * length * head_size),
        compiler_params=pltpu.CompilerParams(vmem_limit_bytes=KERNEL_VMEM),
        name="keep",
    )(tick, in_hbm(stale_key), in_hbm(stale_value))


def attend_body(low, recv_ref, own_ref, kept_key_ref, kept_value_ref, near_ref, far_ref):
    heads, tok_rows, head_size = near_ref.shape
    factor = head_size ** (-0.5) * 1.4426950408889634
    ones = jnp.ones((2 * kept_key_ref.shape[1], head_size), near_ref.dtype)
    for l in range(heads):
        at = low + l
        keys = jnp.concatenate([kept_key_ref[at], own_ref[0, at], recv_ref[0, l]], axis=0)
        values = jnp.concatenate([kept_value_ref[at], own_ref[1, at], recv_ref[1, l]], axis=0)
        queries = jnp.concatenate([own_ref[2, at], recv_ref[2, l]], axis=0)
        scores = lax.dot_general(
            keys, queries, (((1,), (1,)), ((), ())), preferred_element_type=jnp.float32
        )
        top = jnp.max(scores, axis=0, keepdims=True)
        weights = jnp.exp2((scores - top) * factor).astype(near_ref.dtype)
        both = lax.dot_general(
            weights,
            jnp.concatenate([values, ones], axis=1),
            (((0,), (0,)), ((), ())),
            preferred_element_type=jnp.float32,
        )
        result = (both[:, :head_size] / both[:, head_size:]).astype(near_ref.dtype)
        near_ref[l] = result[:tok_rows]
        far_ref[l] = result[tok_rows:]


def attend(low, heads, received, own, kept_key, kept_value):
    tok_rows, head_size = own.shape[2:]
    patch_tok = 2 * tok_rows
    length = MICRO * patch_tok
    out = jax.ShapeDtypeStruct((heads, tok_rows, head_size), own.dtype)
    return pl.pallas_call(
        functools.partial(attend_body, low),
        out_shape=(out, out),
        in_specs=[vmem_space()] * 4,
        out_specs=(vmem_space(),) * 2,
        cost_estimate=pl.CostEstimate(
            flops=6 * heads * patch_tok * length * head_size,
            bytes_accessed=2 * heads * head_size * (2 * length + 2 * patch_tok),
            transcendentals=heads * patch_tok * length,
        ),
        compiler_params=pltpu.CompilerParams(vmem_limit_bytes=KERNEL_VMEM),
        name="attend",
    )(received, own, kept_key, kept_value)


def unpack_body(bounds, order_ref, *refs):
    count = len(bounds)
    near, far = refs[:count], refs[count : 2 * count]
    out_ref, sem = refs[2 * count :]
    me = lax.axis_index("seq")
    head_size = near[0].shape[2]
    for c, (low, heads) in enumerate(bounds):
        for l in range(heads):
            for side, source in ((me, near[c]), (1 - me, far[c])):
                columns = columns_of(order_ref, 2 * (low + l) + side, head_size)
                pltpu.make_async_copy(source.at[l], out_ref.at[0, :, columns], sem).start()
    pltpu.make_async_copy(out_ref, out_ref, sem).wait()


def unpack(bounds, head_order, near, far):
    tok_rows, head_size = near[0].shape[1:]
    shape = (1, tok_rows, head_order.shape[0] * head_size)
    return pl.pallas_call(
        functools.partial(unpack_body, bounds),
        out_shape=jax.ShapeDtypeStruct(shape, near[0].dtype),
        in_specs=[scalar_space()] + [vmem_space()] * (2 * len(bounds)),
        out_specs=hbm_space(),
        scratch_shapes=[pltpu.SemaphoreType.DMA],
        cost_estimate=moved(2 * shape[1] * shape[2]),
        compiler_params=pltpu.CompilerParams(vmem_limit_bytes=KERNEL_VMEM),
        name="unpack",
    )(head_order, *near, *far)


def chunks(heads_dev):
    edges = [round(heads_dev * edge) for edge in EDGES]
    return [(a, b - a) for a, b in zip(edges[:-1], edges[1:])]


def pair_group(query, key_new, value_new, stale_key, stale_value, head_order, tick):
    segments = lax.axis_size("segment")
    bounds = chunks(stale_key.shape[1])
    ahead = [(s, (s + 1) % segments) for s in range(segments)]
    across = [(2 * s + j, 2 * t + 1 - j) for s, t in ahead for j in range(2)]

    order, own, sends = pack(bounds, head_order, query, key_new, value_new)
    received = [lax.ppermute(send, "seq", [(0, 1), (1, 0)]) for send in sends]
    kept_key, kept_value = keep(tick, stale_key, stale_value)
    near, far = [], []
    for (low, heads), got in zip(bounds, received):
        if far:
            got, _ = lax.optimization_barrier((got, theirs))
        ours, theirs = attend(low, heads, got, own, kept_key, kept_value)
        far.append(lax.ppermute(theirs, ("segment", "seq"), across))
        near.append(lax.ppermute(ours, "segment", ahead))
    return unpack(bounds, order, near, far)


def per_device(query, key_new, value_new, stale_key, stale_value, head_order, tick):
    group_size = lax.axis_size("seq")
    heads = head_order.shape[0]
    tok_rows, head_size = query.shape[1], stale_key.shape[3]
    paired = (
        group_size == 2
        and heads == 2 * stale_key.shape[1]
        and stale_key.shape[2] == MICRO * 2 * tok_rows
        and tok_rows % 16 == 0
        and head_size % 128 == 0
    )
    chosen = pair_group if paired else wide_group
    return chosen(query, key_new, value_new, stale_key, stale_value, head_order, tick)


def solution(mesh):
    return jax.shard_map(
        per_device,
        mesh=mesh,
        in_specs=(
            P("segment", ("rep", "seq"), None),
            P("segment", ("rep", "seq"), None),
            P("segment", ("rep", "seq"), None),
            P("segment", ("rep", "seq"), None, None),
            P("segment", ("rep", "seq"), None, None),
            P(),
            P(),
        ),
        out_specs=P("segment", ("rep", "seq"), None),
        check_vma=False,
    )
```

```python
import functools

import jax
import jax.numpy as jnp
from jax import lax
from jax.experimental import pallas as pl
from jax.experimental.pallas import tpu as pltpu
from jax.sharding import PartitionSpec as P

MICRO = 2
EDGES = (0, 0.7, 1)
KERNEL_VMEM = 8 << 20


def from_behind(block, axis, distance):
    devices = range(lax.axis_size(axis))
    route = [((i - distance) % len(devices), i) for i in devices]
    return lax.ppermute(block, axis, route)


def select_table(head_order, group_size, heads_dev):
    head_count = head_order.shape[0]
    slot_ids = (
        jnp.arange(heads_dev, dtype=jnp.int32)[None, :] * group_size
        + jnp.arange(group_size, dtype=jnp.int32)[:, None]
    )
    head_ids = jnp.arange(head_count, dtype=jnp.int32)
    matches = slot_ids[:, :, None] == head_ids[None, None, :]
    head_of = jnp.sum(jnp.where(matches, head_order[None, None, :], 0), axis=-1)
    head_of = jnp.where(slot_ids < head_count, head_of, -1)
    return (head_of[:, :, None] == head_ids[None, None, :]).astype(jnp.bfloat16)


def pack_heads(table, values, head_size):
    rows = values.shape[1]
    per_head = values[0].reshape(rows, table.shape[2], head_size)
    return jnp.einsum("dlh,thc->tdlc", table, per_head, preferred_element_type=jnp.float32).astype(
        jnp.bfloat16
    )


def head_major(received):
    return jnp.transpose(received[:, 0], (1, 0, 2))


def block_count(patch_tok):
    count = max(1, patch_tok // 512)
    while patch_tok % count != 0:
        count = count - 1
    return count


def wide_group(query, key_new, value_new, stale_key, stale_value, head_order, tick):
    group_size = lax.axis_size("seq")
    heads_dev = stale_key.shape[1]
    head_size = stale_key.shape[3]
    tok_rows = query.shape[1]
    patch_tok = tok_rows * group_size
    blocks = block_count(patch_tok)
    block_rows = patch_tok // blocks
    score_scale = head_size ** (-0.5)
    table = select_table(head_order, group_size, heads_dev)
    patch_index = (tick[0] - lax.axis_index("segment")) % MICRO
    first_row = patch_index * patch_tok

    def with_fresh(stale_buf, fresh_rows):
        return lax.dynamic_update_slice(
            stale_buf[0], fresh_rows, (jnp.int32(0), first_row, jnp.int32(0))
        )

    sent_query, sent_key, sent_value = (
        lax.all_to_all(
            pack_heads(table, part, head_size), "seq", split_axis=1, concat_axis=0, tiled=True
        )
        for part in (query, key_new, value_new)
    )
    key_buf = with_fresh(stale_key, head_major(sent_key))
    value_buf = with_fresh(stale_value, head_major(sent_value))

    def attend_full(operands):
        query_blocks, key_rows, value_rows = operands

        def one_block(query_rows):
            scores = (
                jnp.dot(query_rows, key_rows.T, preferred_element_type=jnp.float32) * score_scale
            )
            top = jnp.max(scores, axis=-1, keepdims=True)
            weights = jnp.exp(scores - top).astype(jnp.bfloat16)
            total = jnp.sum(weights, axis=-1, keepdims=True, dtype=jnp.float32)
            numer = jnp.dot(weights, value_rows, preferred_element_type=jnp.float32)
            return (numer / total).astype(jnp.bfloat16)

        return lax.map(one_block, query_blocks).reshape(patch_tok, head_size)

    heads_rows = head_major(sent_query)
    attended = lax.map(
        attend_full,
        (
            heads_rows.reshape(heads_rows.shape[0], blocks, block_rows, heads_rows.shape[-1]),
            key_buf,
            value_buf,
        ),
    )
    outgoing = jnp.transpose(attended, (1, 0, 2))[:, None, :, :]
    returned = lax.all_to_all(outgoing, "seq", split_axis=0, concat_axis=1, tiled=True)
    merged = jnp.einsum(
        "dlh,tdlc->thc", table, returned, preferred_element_type=jnp.float32
    ).astype(jnp.bfloat16)
    result = merged.reshape(1, tok_rows, table.shape[2] * head_size)
    return from_behind(result, "segment", 1)


def hbm_space():
    return pl.BlockSpec(memory_space=pltpu.HBM)


def in_hbm(array):
    return pltpu.with_memory_space_constraint(array, pltpu.HBM)


def vmem_space():
    return pl.BlockSpec(memory_space=pltpu.VMEM)


def scalar_space():
    return pl.BlockSpec(memory_space=pltpu.SMEM)


def columns_of(order_ref, unit, head_size):
    return pl.ds(pl.multiple_of(order_ref[unit] * head_size, head_size), head_size)


def moved(count):
    return pl.CostEstimate(flops=0, bytes_accessed=2 * count, transcendentals=0)


def pack_body(bounds, given_ref, query_ref, key_ref, value_ref, order_ref, fresh_ref, *refs):
    send_refs, (sems,) = refs[: len(bounds)], refs[len(bounds) :]
    other = 1 - lax.axis_index("seq")
    head_size = send_refs[0].shape[3]
    copies = [
        pltpu.make_async_copy(source.at[0], fresh_ref.at[place], sems.at[place])
        for place, source in enumerate((key_ref, value_ref, query_ref))
    ] + [pltpu.make_async_copy(given_ref, order_ref, sems.at[3])]
    for copy in copies:
        copy.start()
    copies[3].wait()
    for place in range(3):
        copies[place].wait()
        for (low, heads), send_ref in zip(bounds, send_refs):
            for l in range(heads):
                columns = columns_of(order_ref, 2 * (low + l) + other, head_size)
                send_ref[place, l] = fresh_ref[place, :, columns]


def pack(bounds, head_order, query, key_new, value_new):
    tok_rows, width = query.shape[1:]
    head_size = width // head_order.shape[0]
    shapes = [
        pltpu.SMEM(head_order.shape, head_order.dtype),
        jax.ShapeDtypeStruct((3, tok_rows, width), query.dtype),
    ] + [
        jax.ShapeDtypeStruct((3, heads, tok_rows, head_size), query.dtype) for _, heads in bounds
    ]
    order, fresh, *sends = pl.pallas_call(
        functools.partial(pack_body, bounds),
        out_shape=shapes,
        in_specs=[hbm_space()] * 4,
        out_specs=[scalar_space()] + [vmem_space()] * (len(shapes) - 1),
        scratch_shapes=[pltpu.SemaphoreType.DMA((4,))],
        cost_estimate=moved(6 * tok_rows * width),
        compiler_params=pltpu.CompilerParams(vmem_limit_bytes=KERNEL_VMEM),
        name="pack",
    )(*(in_hbm(x) for x in (head_order, query, key_new, value_new)))
    return order, fresh, sends


def keep_body(
    order_ref,
    tick_ref,
    fresh_ref,
    stale_key_ref,
    stale_value_ref,
    own_ref,
    key_ref,
    value_ref,
    sems,
):
    me = lax.axis_index("seq")
    patch_tok = key_ref.shape[1]
    head_size = own_ref.shape[3]
    kept = (tick_ref[0] - lax.axis_index("segment") + 1) & 1
    rows = pl.ds(pl.multiple_of(kept * patch_tok, patch_tok), patch_tok)
    copies = [
        pltpu.make_async_copy(source.at[0, :, rows], target, sems.at[i])
        for i, (source, target) in enumerate(
            ((stale_key_ref, key_ref), (stale_value_ref, value_ref))
        )
    ]
    for copy in copies:
        copy.start()
    for l in range(own_ref.shape[1]):
        columns = columns_of(order_ref, 2 * l + me, head_size)
        for place in range(3):
            own_ref[place, l] = fresh_ref[place, :, columns]
    for copy in copies:
        copy.wait()


def keep(order, fresh, tick, stale_key, stale_value):
    _, heads, length, head_size = stale_key.shape
    own = jax.ShapeDtypeStruct((3, heads, fresh.shape[1], head_size), fresh.dtype)
    kept = jax.ShapeDtypeStruct((heads, length // MICRO, head_size), stale_key.dtype)
    return pl.pallas_call(
        keep_body,
        out_shape=(own, kept, kept),
        in_specs=[scalar_space()] * 2 + [vmem_space()] + [hbm_space()] * 2,
        out_specs=(vmem_space(),) * 3,
        scratch_shapes=[pltpu.SemaphoreType.DMA((2,))],
        cost_estimate=moved(2 * heads * length * head_size),
        compiler_params=pltpu.CompilerParams(vmem_limit_bytes=KERNEL_VMEM),
        name="keep",
    )(order, tick, fresh, in_hbm(stale_key), in_hbm(stale_value))


def attend_body(low, recv_ref, own_ref, kept_key_ref, kept_value_ref, first_ref, second_ref):
    odd = (lax.axis_index("segment") & 1) == 1
    heads, tok_rows, head_size = first_ref.shape
    factor = head_size ** (-0.5) * 1.4426950408889634
    ones = jnp.ones((2 * kept_key_ref.shape[1], head_size), first_ref.dtype)
    for l in range(heads):
        at = low + l
        keys = jnp.concatenate([kept_key_ref[at], own_ref[0, at], recv_ref[0, l]], axis=0)
        values = jnp.concatenate([kept_value_ref[at], own_ref[1, at], recv_ref[1, l]], axis=0)
        queries = jnp.concatenate([own_ref[2, at], recv_ref[2, l]], axis=0)
        scores = lax.dot_general(
            keys, queries, (((1,), (1,)), ((), ())), preferred_element_type=jnp.float32
        )
        top = jnp.max(scores, axis=0, keepdims=True)
        weights = jnp.exp2((scores - top) * factor).astype(first_ref.dtype)
        both = lax.dot_general(
            weights,
            jnp.concatenate([values, ones], axis=1),
            (((0,), (0,)), ((), ())),
            preferred_element_type=jnp.float32,
        )
        result = (both[:, :head_size] / both[:, head_size:]).astype(first_ref.dtype)
        first_ref[l] = jnp.where(odd, result[tok_rows:], result[:tok_rows])
        second_ref[l] = jnp.where(odd, result[:tok_rows], result[tok_rows:])


def attend(low, heads, received, own, kept_key, kept_value):
    tok_rows, head_size = own.shape[2:]
    patch_tok = 2 * tok_rows
    length = MICRO * patch_tok
    out = jax.ShapeDtypeStruct((heads, tok_rows, head_size), own.dtype)
    return pl.pallas_call(
        functools.partial(attend_body, low),
        out_shape=(out, out),
        in_specs=[vmem_space()] * 4,
        out_specs=(vmem_space(),) * 2,
        cost_estimate=pl.CostEstimate(
            flops=6 * heads * patch_tok * length * head_size,
            bytes_accessed=2 * heads * head_size * (2 * length + 2 * patch_tok),
            transcendentals=heads * patch_tok * length,
        ),
        compiler_params=pltpu.CompilerParams(vmem_limit_bytes=KERNEL_VMEM),
        name="attend",
    )(received, own, kept_key, kept_value)


def unpack_body(low, order_ref, first_ref, second_ref, *refs):
    out_ref, sems = refs[-2:]
    side = lax.axis_index("seq") ^ ((lax.axis_index("segment") + 1) & 1)
    heads, _, head_size = first_ref.shape
    for l in range(heads):
        for i, (owner, piece) in enumerate(((side, first_ref), (1 - side, second_ref))):
            columns = columns_of(order_ref, 2 * (low + l) + owner, head_size)
            pltpu.make_async_copy(piece.at[l], out_ref.at[0, :, columns], sems.at[i]).start()
    for i, piece in enumerate((first_ref, second_ref)):
        pltpu.make_async_copy(piece, piece, sems.at[i]).wait()


def unpack(low, order, first, second, out):
    heads, tok_rows, head_size = first.shape
    shape = (1, tok_rows, order.shape[0] * head_size)
    return pl.pallas_call(
        functools.partial(unpack_body, low),
        out_shape=pltpu.HBM(shape, first.dtype),
        in_specs=[scalar_space()] + [vmem_space()] * 2 + [hbm_space()] * (out is not None),
        out_specs=hbm_space(),
        input_output_aliases={} if out is None else {3: 0},
        scratch_shapes=[pltpu.SemaphoreType.DMA((2,))],
        cost_estimate=moved(4 * heads * tok_rows * head_size),
        compiler_params=pltpu.CompilerParams(vmem_limit_bytes=KERNEL_VMEM),
        name="unpack",
    )(order, first, second, *(() if out is None else (out,)))


def chunks(heads_dev):
    edges = [round(heads_dev * edge) for edge in EDGES]
    return [(a, b - a) for a, b in zip(edges[:-1], edges[1:])]


def pair_group(query, key_new, value_new, stale_key, stale_value, head_order, tick):
    segments = lax.axis_size("segment")
    bounds = chunks(stale_key.shape[1])

    def handed(block, crossed):
        route = [
            (2 * s + j, 2 * ((s + 1) % segments) + (1 - j if s % 2 == crossed else j))
            for s in range(segments)
            for j in range(2)
        ]
        return lax.ppermute(block, ("segment", "seq"), route)

    order, fresh, sends = pack(bounds, head_order, query, key_new, value_new)
    received = [lax.ppermute(send, "seq", [(0, 1), (1, 0)]) for send in sends]
    own, kept_key, kept_value = keep(order, fresh, tick, stale_key, stale_value)
    results, last = [], None
    for (low, heads), got in zip(bounds, received):
        if last is not None:
            got, _ = lax.optimization_barrier((got, last))
        first, second = attend(low, heads, got, own, kept_key, kept_value)
        last = second
        results.append((low, handed(first, 1), handed(second, 0)))
    out = None
    for low, first, second in results:
        out = unpack(low, order, first, second, out)
    return out


def per_device(query, key_new, value_new, stale_key, stale_value, head_order, tick):
    group_size = lax.axis_size("seq")
    heads = head_order.shape[0]
    tok_rows, head_size = query.shape[1], stale_key.shape[3]
    paired = (
        group_size == 2
        and lax.axis_size("segment") % 2 == 0
        and heads == 2 * stale_key.shape[1]
        and stale_key.shape[2] == MICRO * 2 * tok_rows
        and tok_rows % 16 == 0
        and head_size % 128 == 0
    )
    chosen = pair_group if paired else wide_group
    return chosen(query, key_new, value_new, stale_key, stale_value, head_order, tick)


def solution(mesh):
    return jax.shard_map(
        per_device,
        mesh=mesh,
        in_specs=(
            P("segment", ("rep", "seq"), None),
            P("segment", ("rep", "seq"), None),
            P("segment", ("rep", "seq"), None),
            P("segment", ("rep", "seq"), None, None),
            P("segment", ("rep", "seq"), None, None),
            P(),
            P(),
        ),
        out_specs=P("segment", ("rep", "seq"), None),
        check_vma=False,
    )
```

```python
import functools

import jax
import jax.numpy as jnp
from jax import lax
from jax.experimental import pallas as pl
from jax.experimental.pallas import tpu as pltpu
from jax.sharding import PartitionSpec as P

MICRO = 2
EARLY = 0.75
RULE = (1, 0)
KERNEL_VMEM = 8 << 20


def from_behind(block, axis, distance):
    devices = range(lax.axis_size(axis))
    route = [((i - distance) % len(devices), i) for i in devices]
    return lax.ppermute(block, axis, route)


def select_table(head_order, group_size, heads_dev):
    head_count = head_order.shape[0]
    slot_ids = (
        jnp.arange(heads_dev, dtype=jnp.int32)[None, :] * group_size
        + jnp.arange(group_size, dtype=jnp.int32)[:, None]
    )
    head_ids = jnp.arange(head_count, dtype=jnp.int32)
    matches = slot_ids[:, :, None] == head_ids[None, None, :]
    head_of = jnp.sum(jnp.where(matches, head_order[None, None, :], 0), axis=-1)
    head_of = jnp.where(slot_ids < head_count, head_of, -1)
    return (head_of[:, :, None] == head_ids[None, None, :]).astype(jnp.bfloat16)


def pack_heads(table, values, head_size):
    rows = values.shape[1]
    per_head = values[0].reshape(rows, table.shape[2], head_size)
    return jnp.einsum("dlh,thc->tdlc", table, per_head, preferred_element_type=jnp.float32).astype(
        jnp.bfloat16
    )


def head_major(received):
    return jnp.transpose(received[:, 0], (1, 0, 2))


def block_count(patch_tok):
    count = max(1, patch_tok // 512)
    while patch_tok % count != 0:
        count = count - 1
    return count


def wide_group(query, key_new, value_new, stale_key, stale_value, head_order, tick):
    group_size = lax.axis_size("seq")
    heads_dev = stale_key.shape[1]
    head_size = stale_key.shape[3]
    tok_rows = query.shape[1]
    patch_tok = tok_rows * group_size
    blocks = block_count(patch_tok)
    block_rows = patch_tok // blocks
    score_scale = head_size ** (-0.5)
    table = select_table(head_order, group_size, heads_dev)
    patch_index = (tick[0] - lax.axis_index("segment")) % MICRO
    first_row = patch_index * patch_tok

    def with_fresh(stale_buf, fresh_rows):
        return lax.dynamic_update_slice(
            stale_buf[0], fresh_rows, (jnp.int32(0), first_row, jnp.int32(0))
        )

    sent_query, sent_key, sent_value = (
        lax.all_to_all(
            pack_heads(table, part, head_size), "seq", split_axis=1, concat_axis=0, tiled=True
        )
        for part in (query, key_new, value_new)
    )
    key_buf = with_fresh(stale_key, head_major(sent_key))
    value_buf = with_fresh(stale_value, head_major(sent_value))

    def attend_full(operands):
        query_blocks, key_rows, value_rows = operands

        def one_block(query_rows):
            scores = (
                jnp.dot(query_rows, key_rows.T, preferred_element_type=jnp.float32) * score_scale
            )
            top = jnp.max(scores, axis=-1, keepdims=True)
            weights = jnp.exp(scores - top).astype(jnp.bfloat16)
            total = jnp.sum(weights, axis=-1, keepdims=True, dtype=jnp.float32)
            numer = jnp.dot(weights, value_rows, preferred_element_type=jnp.float32)
            return (numer / total).astype(jnp.bfloat16)

        return lax.map(one_block, query_blocks).reshape(patch_tok, head_size)

    heads_rows = head_major(sent_query)
    attended = lax.map(
        attend_full,
        (
            heads_rows.reshape(heads_rows.shape[0], blocks, block_rows, heads_rows.shape[-1]),
            key_buf,
            value_buf,
        ),
    )
    outgoing = jnp.transpose(attended, (1, 0, 2))[:, None, :, :]
    returned = lax.all_to_all(outgoing, "seq", split_axis=0, concat_axis=1, tiled=True)
    merged = jnp.einsum(
        "dlh,tdlc->thc", table, returned, preferred_element_type=jnp.float32
    ).astype(jnp.bfloat16)
    result = merged.reshape(1, tok_rows, table.shape[2] * head_size)
    return from_behind(result, "segment", 1)


def hbm_space():
    return pl.BlockSpec(memory_space=pltpu.HBM)


def in_hbm(array):
    return pltpu.with_memory_space_constraint(array, pltpu.HBM)


def vmem_space():
    return pl.BlockSpec(memory_space=pltpu.VMEM)


def scalar_space():
    return pl.BlockSpec(memory_space=pltpu.SMEM)


def columns_of(order_ref, unit, head_size):
    return pl.ds(pl.multiple_of(order_ref[unit] * head_size, head_size), head_size)


def moved(count):
    return pl.CostEstimate(flops=0, bytes_accessed=2 * count, transcendentals=0)


def pack_pairs_body(
    heads, given_ref, key_ref, value_ref, order_ref, pairs_ref, send_ref, sems
):
    other = 1 - lax.axis_index("seq")
    head_size = send_ref.shape[3]
    copies = [
        pltpu.make_async_copy(source_ref.at[0], pairs_ref.at[i], sems.at[i])
        for i, source_ref in enumerate((key_ref, value_ref))
    ]
    order_copy = pltpu.make_async_copy(given_ref, order_ref, sems.at[2])
    for copy in copies + [order_copy]:
        copy.start()
    order_copy.wait()
    for i, copy in enumerate(copies):
        copy.wait()
        for l in range(heads):
            send_ref[i, l] = pairs_ref[i, :, columns_of(order_ref, 2 * l + other, head_size)]


def pack_pairs(heads, head_order, key_new, value_new):
    tok_rows, width = key_new.shape[1:]
    head_size = width // head_order.shape[0]
    return pl.pallas_call(
        functools.partial(pack_pairs_body, heads),
        out_shape=(
            pltpu.SMEM(head_order.shape, head_order.dtype),
            jax.ShapeDtypeStruct((2, tok_rows, width), key_new.dtype),
            jax.ShapeDtypeStruct((2, heads, tok_rows, head_size), key_new.dtype),
        ),
        in_specs=[hbm_space()] * 3,
        out_specs=(scalar_space(), vmem_space(), vmem_space()),
        scratch_shapes=[pltpu.SemaphoreType.DMA((3,))],
        cost_estimate=moved(4 * tok_rows * width),
        compiler_params=pltpu.CompilerParams(vmem_limit_bytes=KERNEL_VMEM),
        name="pack_pairs",
    )(in_hbm(head_order), in_hbm(key_new), in_hbm(value_new))


def pack_rest_body(order_ref, pairs_ref, query_ref, fresh_ref, early_ref, late_ref, sem):
    other = 1 - lax.axis_index("seq")
    early, late = early_ref.shape[1], late_ref.shape[1]
    head_size = early_ref.shape[3]
    copy = pltpu.make_async_copy(query_ref.at[0], fresh_ref, sem)
    copy.start()
    for l in range(late):
        columns = columns_of(order_ref, 2 * (early + l) + other, head_size)
        for i in range(2):
            late_ref[i, l] = pairs_ref[i, :, columns]
    copy.wait()
    for l in range(early + late):
        columns = columns_of(order_ref, 2 * l + other, head_size)
        if l < early:
            early_ref[0, l] = fresh_ref[:, columns]
        else:
            late_ref[2, l - early] = fresh_ref[:, columns]


def pack_rest(early, late, order, pairs, query):
    tok_rows, width = query.shape[1:]
    head_size = width // order.shape[0]
    return pl.pallas_call(
        pack_rest_body,
        out_shape=(
            jax.ShapeDtypeStruct((tok_rows, width), query.dtype),
            jax.ShapeDtypeStruct((1, early, tok_rows, head_size), query.dtype),
            jax.ShapeDtypeStruct((3, late, tok_rows, head_size), query.dtype),
        ),
        in_specs=[scalar_space(), vmem_space(), hbm_space()],
        out_specs=(vmem_space(),) * 3,
        scratch_shapes=[pltpu.SemaphoreType.DMA],
        cost_estimate=moved(2 * tok_rows * width),
        compiler_params=pltpu.CompilerParams(vmem_limit_bytes=KERNEL_VMEM),
        name="pack_rest",
    )(order, pairs, in_hbm(query))


def keep_body(
    order_ref,
    tick_ref,
    pairs_ref,
    fresh_ref,
    stale_key_ref,
    stale_value_ref,
    own_ref,
    key_ref,
    value_ref,
    sems,
):
    me = lax.axis_index("seq")
    patch_tok = key_ref.shape[1]
    head_size = own_ref.shape[3]
    kept = (tick_ref[0] - lax.axis_index("segment") + 1) & 1
    rows = pl.ds(pl.multiple_of(kept * patch_tok, patch_tok), patch_tok)
    copies = [
        pltpu.make_async_copy(source.at[0, :, rows], target, sems.at[i])
        for i, (source, target) in enumerate(
            ((stale_key_ref, key_ref), (stale_value_ref, value_ref))
        )
    ]
    for copy in copies:
        copy.start()
    for l in range(own_ref.shape[1]):
        columns = columns_of(order_ref, 2 * l + me, head_size)
        for i in range(2):
            own_ref[i, l] = pairs_ref[i, :, columns]
        own_ref[2, l] = fresh_ref[:, columns]
    for copy in copies:
        copy.wait()


def keep(order, pairs, fresh, tick, stale_key, stale_value):
    _, heads, length, head_size = stale_key.shape
    own = jax.ShapeDtypeStruct((3, heads, fresh.shape[0], head_size), fresh.dtype)
    kept = jax.ShapeDtypeStruct((heads, length // MICRO, head_size), stale_key.dtype)
    return pl.pallas_call(
        keep_body,
        out_shape=(own, kept, kept),
        in_specs=[scalar_space()] * 2 + [vmem_space()] * 2 + [hbm_space()] * 2,
        out_specs=(vmem_space(),) * 3,
        scratch_shapes=[pltpu.SemaphoreType.DMA((2,))],
        cost_estimate=moved(2 * heads * length * head_size),
        compiler_params=pltpu.CompilerParams(vmem_limit_bytes=KERNEL_VMEM),
        name="keep",
    )(order, tick, pairs, fresh, in_hbm(stale_key), in_hbm(stale_value))


def crosses_first(section):
    return jnp.where((section & 1) == 1, RULE[1], RULE[0])


def attend_body(low, outs, recv_ref, query_ref, own_ref, kept_key_ref, kept_value_ref, *out_refs):
    heads, tok_rows, head_size = out_refs[0].shape
    dtype = out_refs[0].dtype
    factor = head_size ** (-0.5) * 1.4426950408889634
    ones = jnp.ones((2 * kept_key_ref.shape[1], head_size), dtype)
    turned = crosses_first(lax.axis_index("segment")) == 1
    for l in range(heads):
        at = low + l
        keys = jnp.concatenate([kept_key_ref[at], own_ref[0, at], recv_ref[0, l]], axis=0)
        values = jnp.concatenate([kept_value_ref[at], own_ref[1, at], recv_ref[1, l]], axis=0)
        queries = {"near": lambda: own_ref[2, at], "far": lambda: query_ref[query_ref.shape[0] - 1, l]}
        queries = jnp.concatenate([queries[out]() for out in outs], axis=0)
        scores = lax.dot_general(
            keys, queries, (((1,), (1,)), ((), ())), preferred_element_type=jnp.float32
        )
        top = jnp.max(scores, axis=0, keepdims=True)
        weights = jnp.exp2((scores - top) * factor).astype(dtype)
        both = lax.dot_general(
            weights,
            jnp.concatenate([values, ones], axis=1),
            (((0,), (0,)), ((), ())),
            preferred_element_type=jnp.float32,
        )
        result = (both[:, :head_size] / both[:, head_size:]).astype(dtype)
        if len(outs) == 1:
            out_refs[0][l] = result
        else:
            out_refs[0][l] = jnp.where(turned, result[tok_rows:], result[:tok_rows])
            out_refs[1][l] = jnp.where(turned, result[:tok_rows], result[tok_rows:])


def attend(low, heads, outs, received, queries, own, kept_key, kept_value):
    tok_rows, head_size = own.shape[2:]
    rows = len(outs) * tok_rows
    length = 2 * MICRO * tok_rows
    out = jax.ShapeDtypeStruct((heads, tok_rows, head_size), own.dtype)
    return pl.pallas_call(
        functools.partial(attend_body, low, outs),
        out_shape=(out,) * len(outs),
        in_specs=[vmem_space()] * 5,
        out_specs=(vmem_space(),) * len(outs),
        cost_estimate=pl.CostEstimate(
            flops=6 * heads * rows * length * head_size,
            bytes_accessed=2 * heads * head_size * (2 * length + 2 * rows),
            transcendentals=heads * rows * length,
        ),
        compiler_params=pltpu.CompilerParams(vmem_limit_bytes=KERNEL_VMEM),
        name="attend",
    )(received, queries, own, kept_key, kept_value)


def unpack_body(low, turns, order_ref, *refs):
    pieces, (out_ref, sems) = refs[:2], refs[-2:]
    side = lax.axis_index("seq")
    if turns:
        side = side ^ crosses_first(lax.axis_index("segment") + 1)
    heads, _, head_size = pieces[0].shape
    for l in range(heads):
        for i, piece in enumerate(pieces):
            columns = columns_of(order_ref, 2 * (low + l) + (side ^ i), head_size)
            pltpu.make_async_copy(piece.at[l], out_ref.at[0, :, columns], sems.at[i]).start()
    for i, piece in enumerate(pieces):
        pltpu.make_async_copy(piece, piece, sems.at[i]).wait()


def unpack(low, turns, order, pieces, out):
    heads, tok_rows, head_size = pieces[0].shape
    shape = (1, tok_rows, order.shape[0] * head_size)
    return pl.pallas_call(
        functools.partial(unpack_body, low, turns),
        out_shape=pltpu.HBM(shape, pieces[0].dtype),
        in_specs=[scalar_space()] + [vmem_space()] * 2 + [hbm_space()] * (out is not None),
        out_specs=hbm_space(),
        input_output_aliases={} if out is None else {3: 0},
        scratch_shapes=[pltpu.SemaphoreType.DMA((2,))],
        cost_estimate=moved(4 * heads * tok_rows * head_size),
        compiler_params=pltpu.CompilerParams(vmem_limit_bytes=KERNEL_VMEM),
        name="unpack",
    )(order, *pieces, *(() if out is None else (out,)))


def pair_group(query, key_new, value_new, stale_key, stale_value, head_order, tick):
    segments = lax.axis_size("segment")
    heads_dev = stale_key.shape[1]
    early = round(heads_dev * EARLY)
    late = heads_dev - early

    def swap(block):
        return lax.ppermute(block, "seq", [(0, 1), (1, 0)])

    def hand_on(block, rule):
        route = [
            (2 * s + j, 2 * ((s + 1) % segments) + (1 - j if rule[s % 2] else j))
            for s in range(segments)
            for j in range(2)
        ]
        return lax.ppermute(block, ("segment", "seq"), route)

    def after(block, other):
        return lax.optimization_barrier((block, other))[0]

    order, pairs, send = pack_pairs(early, head_order, key_new, value_new)
    early_pairs = swap(send)
    fresh, *sends = pack_rest(early, late, order, pairs, query)
    early_queries, late_all = (swap(send) for send in sends)
    held = keep(order, pairs, fresh, tick, stale_key, stale_value)
    (near,) = attend(0, early, ("near",), early_pairs, early_pairs, *held)
    near_early = hand_on(near, (0, 0))
    early_queries = after(early_queries, near)
    (far,) = attend(0, early, ("far",), early_pairs, early_queries, *held)
    far_early = hand_on(far, (1, 1))
    late_all = after(after(late_all, far), near_early)
    first, second = attend(early, late, ("near", "far"), late_all, late_all, *held)
    first, second = hand_on(first, RULE), hand_on(second, [1 - r for r in RULE])
    out = unpack(0, False, order, (near_early, far_early), None)
    return unpack(early, True, order, (first, second), out)


def per_device(query, key_new, value_new, stale_key, stale_value, head_order, tick):
    group_size = lax.axis_size("seq")
    heads = head_order.shape[0]
    tok_rows, head_size = query.shape[1], stale_key.shape[3]
    paired = (
        group_size == 2
        and lax.axis_size("segment") % 2 == 0
        and heads == 2 * stale_key.shape[1]
        and stale_key.shape[2] == MICRO * 2 * tok_rows
        and tok_rows % 16 == 0
        and head_size % 128 == 0
    )
    chosen = pair_group if paired else wide_group
    return chosen(query, key_new, value_new, stale_key, stale_value, head_order, tick)


def solution(mesh):
    return jax.shard_map(
        per_device,
        mesh=mesh,
        in_specs=(
            P("segment", ("rep", "seq"), None),
            P("segment", ("rep", "seq"), None),
            P("segment", ("rep", "seq"), None),
            P("segment", ("rep", "seq"), None, None),
            P("segment", ("rep", "seq"), None, None),
            P(),
            P(),
        ),
        out_specs=P("segment", ("rep", "seq"), None),
        check_vma=False,
    )
```

```python
import functools

import jax
import jax.numpy as jnp
from jax import lax
from jax.experimental import pallas as pl
from jax.experimental.pallas import tpu as pltpu
from jax.sharding import PartitionSpec as P

MICRO = 2
EARLY = 0.75
RULE = (1, 0)
KERNEL_VMEM = 8 << 20


def from_behind(block, axis, distance):
    devices = range(lax.axis_size(axis))
    route = [((i - distance) % len(devices), i) for i in devices]
    return lax.ppermute(block, axis, route)


def select_table(head_order, group_size, heads_dev):
    head_count = head_order.shape[0]
    slot_ids = (
        jnp.arange(heads_dev, dtype=jnp.int32)[None, :] * group_size
        + jnp.arange(group_size, dtype=jnp.int32)[:, None]
    )
    head_ids = jnp.arange(head_count, dtype=jnp.int32)
    matches = slot_ids[:, :, None] == head_ids[None, None, :]
    head_of = jnp.sum(jnp.where(matches, head_order[None, None, :], 0), axis=-1)
    head_of = jnp.where(slot_ids < head_count, head_of, -1)
    return (head_of[:, :, None] == head_ids[None, None, :]).astype(jnp.bfloat16)


def pack_heads(table, values, head_size):
    rows = values.shape[1]
    per_head = values[0].reshape(rows, table.shape[2], head_size)
    return jnp.einsum("dlh,thc->tdlc", table, per_head, preferred_element_type=jnp.float32).astype(
        jnp.bfloat16
    )


def head_major(received):
    return jnp.transpose(received[:, 0], (1, 0, 2))


def block_count(patch_tok):
    count = max(1, patch_tok // 512)
    while patch_tok % count != 0:
        count = count - 1
    return count


def wide_group(query, key_new, value_new, stale_key, stale_value, head_order, tick):
    group_size = lax.axis_size("seq")
    heads_dev = stale_key.shape[1]
    head_size = stale_key.shape[3]
    tok_rows = query.shape[1]
    patch_tok = tok_rows * group_size
    blocks = block_count(patch_tok)
    block_rows = patch_tok // blocks
    score_scale = head_size ** (-0.5)
    table = select_table(head_order, group_size, heads_dev)
    patch_index = (tick[0] - lax.axis_index("segment")) % MICRO
    first_row = patch_index * patch_tok

    def with_fresh(stale_buf, fresh_rows):
        return lax.dynamic_update_slice(
            stale_buf[0], fresh_rows, (jnp.int32(0), first_row, jnp.int32(0))
        )

    sent_query, sent_key, sent_value = (
        lax.all_to_all(
            pack_heads(table, part, head_size), "seq", split_axis=1, concat_axis=0, tiled=True
        )
        for part in (query, key_new, value_new)
    )
    key_buf = with_fresh(stale_key, head_major(sent_key))
    value_buf = with_fresh(stale_value, head_major(sent_value))

    def attend_full(operands):
        query_blocks, key_rows, value_rows = operands

        def one_block(query_rows):
            scores = (
                jnp.dot(query_rows, key_rows.T, preferred_element_type=jnp.float32) * score_scale
            )
            top = jnp.max(scores, axis=-1, keepdims=True)
            weights = jnp.exp(scores - top).astype(jnp.bfloat16)
            total = jnp.sum(weights, axis=-1, keepdims=True, dtype=jnp.float32)
            numer = jnp.dot(weights, value_rows, preferred_element_type=jnp.float32)
            return (numer / total).astype(jnp.bfloat16)

        return lax.map(one_block, query_blocks).reshape(patch_tok, head_size)

    heads_rows = head_major(sent_query)
    attended = lax.map(
        attend_full,
        (
            heads_rows.reshape(heads_rows.shape[0], blocks, block_rows, heads_rows.shape[-1]),
            key_buf,
            value_buf,
        ),
    )
    outgoing = jnp.transpose(attended, (1, 0, 2))[:, None, :, :]
    returned = lax.all_to_all(outgoing, "seq", split_axis=0, concat_axis=1, tiled=True)
    merged = jnp.einsum(
        "dlh,tdlc->thc", table, returned, preferred_element_type=jnp.float32
    ).astype(jnp.bfloat16)
    result = merged.reshape(1, tok_rows, table.shape[2] * head_size)
    return from_behind(result, "segment", 1)


def hbm_space():
    return pl.BlockSpec(memory_space=pltpu.HBM)


def in_hbm(array):
    return pltpu.with_memory_space_constraint(array, pltpu.HBM)


def vmem_space():
    return pl.BlockSpec(memory_space=pltpu.VMEM)


def scalar_space():
    return pl.BlockSpec(memory_space=pltpu.SMEM)


def columns_of(order_ref, unit, head_size):
    return pl.ds(pl.multiple_of(order_ref[unit] * head_size, head_size), head_size)


def moved(count):
    return pl.CostEstimate(flops=0, bytes_accessed=2 * count, transcendentals=0)


def pack_keys_body(given_ref, key_ref, order_ref, fresh_ref, send_ref, sems):
    other = 1 - lax.axis_index("seq")
    _, heads, _, head_size = send_ref.shape
    order_copy = pltpu.make_async_copy(given_ref, order_ref, sems.at[1])
    copy = pltpu.make_async_copy(key_ref.at[0], fresh_ref, sems.at[0])
    copy.start()
    order_copy.start()
    order_copy.wait()
    copy.wait()
    for l in range(heads):
        send_ref[0, l] = fresh_ref[:, columns_of(order_ref, 2 * l + other, head_size)]


def pack_keys(heads, head_order, key_new):
    tok_rows, width = key_new.shape[1:]
    head_size = width // head_order.shape[0]
    return pl.pallas_call(
        pack_keys_body,
        out_shape=(
            pltpu.SMEM(head_order.shape, head_order.dtype),
            jax.ShapeDtypeStruct((tok_rows, width), key_new.dtype),
            jax.ShapeDtypeStruct((1, heads, tok_rows, head_size), key_new.dtype),
        ),
        in_specs=[hbm_space()] * 2,
        out_specs=(scalar_space(), vmem_space(), vmem_space()),
        scratch_shapes=[pltpu.SemaphoreType.DMA((2,))],
        cost_estimate=moved(2 * tok_rows * width),
        compiler_params=pltpu.CompilerParams(vmem_limit_bytes=KERNEL_VMEM),
        name="pack_keys",
    )(in_hbm(head_order), in_hbm(key_new))


def pack_rest_body(
    order_ref, keys_ref, value_ref, query_ref, fresh_ref, values_ref, queries_ref, late_ref, sems
):
    other = 1 - lax.axis_index("seq")
    early, late = values_ref.shape[1], late_ref.shape[1]
    head_size = late_ref.shape[3]
    copies = [
        pltpu.make_async_copy(source_ref.at[0], fresh_ref.at[i], sems.at[i])
        for i, source_ref in enumerate((value_ref, query_ref))
    ]
    for copy in copies:
        copy.start()
    for l in range(late):
        columns = columns_of(order_ref, 2 * (early + l) + other, head_size)
        late_ref[0, l] = keys_ref[:, columns]
    for i, target_ref in enumerate((values_ref, queries_ref)):
        copies[i].wait()
        for l in range(early + late):
            columns = columns_of(order_ref, 2 * l + other, head_size)
            if l < early:
                target_ref[0, l] = fresh_ref[i, :, columns]
            else:
                late_ref[1 + i, l - early] = fresh_ref[i, :, columns]


def pack_rest(early, late, order, keys, value_new, query):
    tok_rows, width = query.shape[1:]
    head_size = width // order.shape[0]
    sent = jax.ShapeDtypeStruct((1, early, tok_rows, head_size), query.dtype)
    return pl.pallas_call(
        pack_rest_body,
        out_shape=(
            jax.ShapeDtypeStruct((2, tok_rows, width), query.dtype),
            sent,
            sent,
            jax.ShapeDtypeStruct((3, late, tok_rows, head_size), query.dtype),
        ),
        in_specs=[scalar_space(), vmem_space()] + [hbm_space()] * 2,
        out_specs=(vmem_space(),) * 4,
        scratch_shapes=[pltpu.SemaphoreType.DMA((2,))],
        cost_estimate=moved(4 * tok_rows * width),
        compiler_params=pltpu.CompilerParams(vmem_limit_bytes=KERNEL_VMEM),
        name="pack_rest",
    )(order, keys, in_hbm(value_new), in_hbm(query))


def keep_body(
    order_ref,
    tick_ref,
    keys_ref,
    fresh_ref,
    stale_key_ref,
    stale_value_ref,
    own_ref,
    key_ref,
    value_ref,
    sems,
):
    me = lax.axis_index("seq")
    patch_tok = key_ref.shape[1]
    head_size = own_ref.shape[3]
    kept = (tick_ref[0] - lax.axis_index("segment") + 1) & 1
    rows = pl.ds(pl.multiple_of(kept * patch_tok, patch_tok), patch_tok)
    copies = [
        pltpu.make_async_copy(source.at[0, :, rows], target, sems.at[i])
        for i, (source, target) in enumerate(
            ((stale_key_ref, key_ref), (stale_value_ref, value_ref))
        )
    ]
    for copy in copies:
        copy.start()
    for l in range(own_ref.shape[1]):
        columns = columns_of(order_ref, 2 * l + me, head_size)
        own_ref[0, l] = keys_ref[:, columns]
        for i in range(2):
            own_ref[1 + i, l] = fresh_ref[i, :, columns]
    for copy in copies:
        copy.wait()


def keep(order, keys, fresh, tick, stale_key, stale_value):
    _, heads, length, head_size = stale_key.shape
    own = jax.ShapeDtypeStruct((3, heads, fresh.shape[1], head_size), fresh.dtype)
    kept = jax.ShapeDtypeStruct((heads, length // MICRO, head_size), stale_key.dtype)
    return pl.pallas_call(
        keep_body,
        out_shape=(own, kept, kept),
        in_specs=[scalar_space()] * 2 + [vmem_space()] * 2 + [hbm_space()] * 2,
        out_specs=(vmem_space(),) * 3,
        scratch_shapes=[pltpu.SemaphoreType.DMA((2,))],
        cost_estimate=moved(2 * heads * length * head_size),
        compiler_params=pltpu.CompilerParams(vmem_limit_bytes=KERNEL_VMEM),
        name="keep",
    )(order, tick, keys, fresh, in_hbm(stale_key), in_hbm(stale_value))


def crosses_first(section):
    return jnp.where((section & 1) == 1, RULE[1], RULE[0])


def attend_body(low, outs, recv_key_ref, recv_value_ref, query_ref, own_ref, kept_key_ref, kept_value_ref, *out_refs):
    heads, tok_rows, head_size = out_refs[0].shape
    dtype = out_refs[0].dtype
    factor = head_size ** (-0.5) * 1.4426950408889634
    ones = jnp.ones((2 * kept_key_ref.shape[1], head_size), dtype)
    turned = crosses_first(lax.axis_index("segment")) == 1
    for l in range(heads):
        at = low + l
        keys = jnp.concatenate([kept_key_ref[at], own_ref[0, at], recv_key_ref[0, l]], axis=0)
        values = jnp.concatenate([kept_value_ref[at], own_ref[1, at], recv_value_ref[recv_value_ref.shape[0] // 2, l]], axis=0)
        queries = {"near": lambda: own_ref[2, at], "far": lambda: query_ref[query_ref.shape[0] - 1, l]}
        queries = jnp.concatenate([queries[out]() for out in outs], axis=0)
        scores = lax.dot_general(
            keys, queries, (((1,), (1,)), ((), ())), preferred_element_type=jnp.float32
        )
        top = jnp.max(scores, axis=0, keepdims=True)
        weights = jnp.exp2((scores - top) * factor).astype(dtype)
        both = lax.dot_general(
            weights,
            jnp.concatenate([values, ones], axis=1),
            (((0,), (0,)), ((), ())),
            preferred_element_type=jnp.float32,
        )
        result = (both[:, :head_size] / both[:, head_size:]).astype(dtype)
        if len(outs) == 1:
            out_refs[0][l] = result
        else:
            out_refs[0][l] = jnp.where(turned, result[tok_rows:], result[:tok_rows])
            out_refs[1][l] = jnp.where(turned, result[:tok_rows], result[tok_rows:])


def attend(low, heads, outs, keys, values, queries, own, kept_key, kept_value):
    tok_rows, head_size = own.shape[2:]
    rows = len(outs) * tok_rows
    length = 2 * MICRO * tok_rows
    out = jax.ShapeDtypeStruct((heads, tok_rows, head_size), own.dtype)
    return pl.pallas_call(
        functools.partial(attend_body, low, outs),
        out_shape=(out,) * len(outs),
        in_specs=[vmem_space()] * 6,
        out_specs=(vmem_space(),) * len(outs),
        cost_estimate=pl.CostEstimate(
            flops=6 * heads * rows * length * head_size,
            bytes_accessed=2 * heads * head_size * (2 * length + 2 * rows),
            transcendentals=heads * rows * length,
        ),
        compiler_params=pltpu.CompilerParams(vmem_limit_bytes=KERNEL_VMEM),
        name="attend",
    )(keys, values, queries, own, kept_key, kept_value)


def unpack_body(low, turns, order_ref, *refs):
    pieces, (out_ref, sems) = refs[:2], refs[-2:]
    side = lax.axis_index("seq")
    if turns:
        side = side ^ crosses_first(lax.axis_index("segment") + 1)
    heads, _, head_size = pieces[0].shape
    for l in range(heads):
        for i, piece in enumerate(pieces):
            columns = columns_of(order_ref, 2 * (low + l) + (side ^ i), head_size)
            pltpu.make_async_copy(piece.at[l], out_ref.at[0, :, columns], sems.at[i]).start()
    for i, piece in enumerate(pieces):
        pltpu.make_async_copy(piece, piece, sems.at[i]).wait()


def unpack(low, turns, order, pieces, out):
    heads, tok_rows, head_size = pieces[0].shape
    shape = (1, tok_rows, order.shape[0] * head_size)
    return pl.pallas_call(
        functools.partial(unpack_body, low, turns),
        out_shape=pltpu.HBM(shape, pieces[0].dtype),
        in_specs=[scalar_space()] + [vmem_space()] * 2 + [hbm_space()] * (out is not None),
        out_specs=hbm_space(),
        input_output_aliases={} if out is None else {3: 0},
        scratch_shapes=[pltpu.SemaphoreType.DMA((2,))],
        cost_estimate=moved(4 * heads * tok_rows * head_size),
        compiler_params=pltpu.CompilerParams(vmem_limit_bytes=KERNEL_VMEM),
        name="unpack",
    )(order, *pieces, *(() if out is None else (out,)))


def pair_group(query, key_new, value_new, stale_key, stale_value, head_order, tick):
    segments = lax.axis_size("segment")
    heads_dev = stale_key.shape[1]
    early = round(heads_dev * EARLY)
    late = heads_dev - early

    def swap(block):
        return lax.ppermute(block, "seq", [(0, 1), (1, 0)])

    def hand_on(block, rule):
        route = [
            (2 * s + j, 2 * ((s + 1) % segments) + (1 - j if rule[s % 2] else j))
            for s in range(segments)
            for j in range(2)
        ]
        return lax.ppermute(block, ("segment", "seq"), route)

    def after(block, other):
        return lax.optimization_barrier((block, other))[0]

    order, keys, send = pack_keys(early, head_order, key_new)
    early_keys = swap(send)
    fresh, *sends = pack_rest(early, late, order, keys, value_new, query)
    early_values, early_queries, late_all = (swap(send) for send in sends)
    held = keep(order, keys, fresh, tick, stale_key, stale_value)
    early_pairs = (early_keys, early_values)
    (near,) = attend(0, early, ("near",), *early_pairs, early_values, *held)
    near_early = hand_on(near, (0, 0))
    early_queries = after(early_queries, near)
    (far,) = attend(0, early, ("far",), *early_pairs, early_queries, *held)
    far_early = hand_on(far, (1, 1))
    late_all = after(after(late_all, far), near_early)
    first, second = attend(early, late, ("near", "far"), *[late_all] * 3, *held)
    first, second = hand_on(first, RULE), hand_on(second, [1 - r for r in RULE])
    out = unpack(0, False, order, (near_early, far_early), None)
    return unpack(early, True, order, (first, second), out)


def per_device(query, key_new, value_new, stale_key, stale_value, head_order, tick):
    group_size = lax.axis_size("seq")
    heads = head_order.shape[0]
    tok_rows, head_size = query.shape[1], stale_key.shape[3]
    paired = (
        group_size == 2
        and lax.axis_size("segment") % 2 == 0
        and heads == 2 * stale_key.shape[1]
        and stale_key.shape[2] == MICRO * 2 * tok_rows
        and tok_rows % 16 == 0
        and head_size % 128 == 0
    )
    chosen = pair_group if paired else wide_group
    return chosen(query, key_new, value_new, stale_key, stale_value, head_order, tick)


def solution(mesh):
    return jax.shard_map(
        per_device,
        mesh=mesh,
        in_specs=(
            P("segment", ("rep", "seq"), None),
            P("segment", ("rep", "seq"), None),
            P("segment", ("rep", "seq"), None),
            P("segment", ("rep", "seq"), None, None),
            P("segment", ("rep", "seq"), None, None),
            P(),
            P(),
        ),
        out_specs=P("segment", ("rep", "seq"), None),
        check_vma=False,
    )
```
